32 devices in a mesh: clu: 8 (over z, y), sub: 4 (over x, core).
Axes of the slice: x: 2, y: 2, z: 4, core: 2. Of those that a mesh axis runs over, the one named last changes fastest.
Arguments:
- points: bfloat16 [256, 1024, 128], P('clu', 'sub'), may hold values from -6 to 6
- row_sketch: bfloat16 [8, 8, 1024, 128], P('clu', 'sub'), may hold values from -0.75 to 0.75
- col_sketch: bfloat16 [8, 8, 1024, 128], P('clu', 'sub'), may hold values from -0.75 to 0.75
- pair_count: int32 [8], P('clu'), may hold values from 1 to 8
- pair_local: int32 [8, 8], P('clu'), may hold values from 0 to 31
- pair_src: int32 [8, 8], P('clu'), may hold values from 0 to 7, as said below
- pair_partner: int32 [8, 8], P('clu'), may hold values from 0 to 31
- pair_rank: int32 [8, 8], P('clu'), may hold values from 64 to 128
Outputs:
- row_factor: bfloat16 [8, 8, 1024, 128], P('clu', 'sub')
- col_factor: bfloat16 [8, 8, 2, 1024, 128], P('clu', None, None, 'sub')
The draws below stay inside these ranges and needn't reach their ends.
Inputs may be any that keep to these rules, and one draw needn't show every extreme that they name: `pair_src`: in each group's row every source group appears exactly 2 times or not at all, and its 2 slots p lie in 2 different blocks p // 2.
All inputs are finite; a program needn't handle non-finite values.
Results may differ from the reference program's by a relative error of at most 0.0049.
Values may be sent and summed in bfloat16 or wider, within the bound.
No kernel may reach another device: no remote copies, remote signals or barrier semaphores. Data moves between devices by JAX's collectives and lax.ppermute only.
A program may use at most 128 MiB of HBM per device.

```python
import jax
import jax.numpy as jnp
from jax import lax

DIM = 128
CLS = 1024
RMAX = 128
CAP = 2
CPG = 32
GROUPS = 8
PAIRS = 8
PQ = 2
CLUSTERS = 256
N_SUB = 4


def draw_pair_src(key, part):
    row_keys = jax.random.split(jax.random.fold_in(key, 11), GROUPS)

    def one_row(row_key):
        first_key, second_key, third_key = jax.random.split(row_key, 3)
        chosen = jax.random.permutation(first_key, GROUPS)[:PAIRS // CAP]
        laid = jnp.concatenate([chosen] * CAP).reshape(N_SUB, PQ)
        column_keys = jax.random.split(second_key, N_SUB)
        mixed = jax.vmap(lambda one_key, one_line: one_line[jax.random.permutation(one_key, PQ)])(column_keys, laid)
        mixed = mixed[jax.random.permutation(third_key, N_SUB)]
        return mixed.reshape(PAIRS)
    return jax.vmap(one_row)(row_keys).astype(jnp.int32)


def place_ends(drawn, key, least, high):
    spot = [jax.random.randint(jax.random.fold_in(key, axis), (), 0, length) for axis, length in enumerate(drawn.shape)]
    widest = drawn.shape.index(max(drawn.shape))
    neighbour = spot[:widest] + [(spot[widest] + 1) % drawn.shape[widest]] + spot[widest + 1:]
    return drawn.at[tuple(spot)].set(least).at[tuple(neighbour)].set(high)


def shard_levels(own_key, extent, cuts, smallest, top_value):
    def one(dim, blocks):
        draws = jax.random.uniform(jax.random.fold_in(jax.random.fold_in(own_key, 6), dim), (blocks,), jnp.float32, smallest / len(cuts), top_value / len(cuts))
        return jnp.repeat(jnp.exp(draws), extent[dim] // blocks).reshape((-1,) + (1,) * (len(extent) - dim - 1))

    loudness = one(*cuts[0])
    for cut in cuts[1:]:
        loudness = loudness * one(*cut)
    return loudness


def noise(own_key, extent, spread, most, shards=(), held_as=jnp.bfloat16):
    gain = shard_levels(own_key, extent, shards, -0.22, 0.18) if shards else 1.0
    values = jax.random.normal(own_key, extent, jnp.float32) * spread * gain
    return jnp.minimum(jnp.maximum(values, -most), most).astype(held_as)


def setup_inputs(seed: int = 0) -> dict:
    seeds = jax.random.split(jax.random.key(seed), 9)
    return {
        "points": noise(seeds[0], (CLUSTERS, CLS, DIM), 1.0, 6.0, ((0, 8), (1, 4))),
        "row_sketch": noise(seeds[1], (GROUPS, PAIRS, CLS, RMAX), (CLS // 16) ** -0.5, 0.75, ((0, 8), (1, 4))),
        "col_sketch": noise(seeds[2], (GROUPS, PAIRS, CLS, RMAX), (CLS // 16) ** -0.5, 0.75, ((0, 8), (1, 4))),
        "pair_count": place_ends(jax.random.randint(seeds[3], (GROUPS,), GROUPS // 8, GROUPS + 1), jax.random.fold_in(seeds[3], 1), GROUPS // 8, GROUPS).astype(jnp.int32),
        "pair_local": place_ends(jax.random.randint(seeds[4], (GROUPS, PAIRS), 0, CPG), jax.random.fold_in(seeds[4], 1), 0, CPG - 1).astype(jnp.int32),
        "pair_src": draw_pair_src(jax.random.fold_in(seeds[8], 71), 0),
        "pair_partner": place_ends(jax.random.randint(seeds[6], (GROUPS, PAIRS), 0, CPG), jax.random.fold_in(seeds[6], 1), 0, CPG - 1).astype(jnp.int32),
        "pair_rank": place_ends(jax.random.randint(seeds[7], (GROUPS, PAIRS), RMAX // 2, RMAX + 1), jax.random.fold_in(seeds[7], 1), RMAX // 2, RMAX).astype(jnp.int32),
    }


def kernel_tile(left_points, right_points):
    left_norm = jnp.sum(jnp.square(left_points.astype(jnp.float32)), axis=1)
    right_norm = jnp.sum(jnp.square(right_points.astype(jnp.float32)), axis=1)
    inner_term = jnp.dot(left_points, right_points.T, preferred_element_type=jnp.float32)
    return jnp.exp(-(left_norm[:, None] + right_norm[None, :] - 2.0 * inner_term) / DIM)


def slot_numbers(sources):
    position = jnp.arange(sources.shape[0], dtype=jnp.int32)
    earlier_same = (sources[:, None] == sources[None, :]) & (position[None, :] < position[:, None])
    return jnp.sum(earlier_same.astype(jnp.int32), axis=1).astype(jnp.int32)


def reference(points, row_sketch, col_sketch, pair_count, pair_local, pair_src, pair_partner, pair_rank):
    slot_index = jax.vmap(slot_numbers)(pair_src)
    group_grid = jnp.broadcast_to(jnp.arange(GROUPS, dtype=jnp.int32)[:, None], (GROUPS, PAIRS))
    pair_grid = jnp.broadcast_to(jnp.arange(PAIRS, dtype=jnp.int32)[None, :], (GROUPS, PAIRS))

    def one_pair(pair_item):
        group_id, pair_id = pair_item
        source = pair_src[group_id, pair_id]
        owner_pts = points[group_id * CPG + pair_local[group_id, pair_id]]
        partner_pts = points[source * CPG + pair_partner[group_id, pair_id]]
        kernel_block = kernel_tile(owner_pts, partner_pts).astype(jnp.bfloat16)
        live_cols = (pair_id < pair_count[group_id]) & (jnp.arange(RMAX, dtype=jnp.int32) < pair_rank[group_id, pair_id])
        keep_mask = live_cols.astype(jnp.float32)
        row_part = jnp.dot(kernel_block, row_sketch[group_id, pair_id], preferred_element_type=jnp.float32) * keep_mask
        col_part = jnp.dot(kernel_block.T, col_sketch[group_id, pair_id], preferred_element_type=jnp.float32) * keep_mask
        return row_part.astype(jnp.bfloat16), col_part.astype(jnp.bfloat16)

    row_part, col_part = lax.map(one_pair, (group_grid.reshape(-1), pair_grid.reshape(-1)))
    row_factor = row_part.reshape(GROUPS, PAIRS, CLS, RMAX)
    col_factor = jnp.zeros((GROUPS, GROUPS, CAP, CLS, RMAX), jnp.bfloat16)
    col_factor = col_factor.at[pair_src.reshape(-1), group_grid.reshape(-1), slot_index.reshape(-1)].set(col_part)
    return row_factor, col_factor
```

```python
import functools

import jax
import jax.numpy as jnp
from jax import lax
from jax.experimental import pallas as pl
from jax.experimental.pallas import tpu as pltpu
from jax.sharding import PartitionSpec as P


CAP = 2

SMEM = pl.BlockSpec(memory_space=pltpu.SMEM)
ANY = pl.BlockSpec(memory_space=pl.ANY)
NT = (((1,), (1,)), ((), ()))


def norm_row(x):
    wide = x.astype(jnp.float32)
    square = wide * wide
    high = square.astype(jnp.bfloat16)
    low = (square - high.astype(jnp.float32)).astype(jnp.bfloat16)
    ones = jnp.ones((16, x.shape[1]), jnp.bfloat16)
    return (
        lax.dot_general(ones, high, NT, preferred_element_type=jnp.float32)
        + lax.dot_general(ones, low, NT, preferred_element_type=jnp.float32)
    )[0:1]


def norm_column(x):
    wide = x.astype(jnp.float32)
    return jnp.sum(wide * wide, axis=1, keepdims=True)


def tile_of(left, right):
    inner = lax.dot_general(left, right, NT, preferred_element_type=jnp.float32)
    spread = norm_column(left) + norm_row(right) - 2.0 * inner
    return jnp.exp(spread * (-1.0 / left.shape[1])).astype(jnp.bfloat16)


def copy_all(steps):
    ins = [pltpu.make_async_copy(a, b, s) for a, b, _, s, _ in steps]
    outs = [pltpu.make_async_copy(b, c, s) for _, b, c, _, s in steps]
    for c in ins:
        c.start()
    for i, o in zip(ins, outs):
        i.wait()
        o.start()
    for o in outs:
        o.wait()


def table_kernel(groups, src, count, rank, pair_at, live, seen):
    def clear(g, _):
        seen[g] = 0
        for c in range(CAP):
            pair_at[g, c] = -1
        return 0

    lax.fori_loop(0, groups, clear, 0)

    def one(p, _):
        g = src[0, p]
        c = seen[g]
        seen[g] = c + 1
        pair_at[g, c] = p
        live[p] = jnp.where(p < count[0], rank[0, p], 0)
        return 0

    lax.fori_loop(0, src.shape[1], one, 0)


def prep_kernel(where, local, points, row_sketch, strips, parts, vstrips, vparts, in_sem, out_sem):
    pairs, rows, _ = strips.shape
    steps = []
    for p in range(pairs):
        steps.append((points.at[local[0, p]], vstrips.at[p], strips.at[p], in_sem.at[p], out_sem.at[p]))
    for half in range(parts.shape[0]):
        i = pairs + half
        spot = jnp.bitwise_xor(where[1], 1 + 2 * half)
        span = pl.ds(pl.multiple_of(spot * rows, rows), rows)
        steps.append((row_sketch.at[0, :, span], vparts.at[half], parts.at[half], in_sem.at[i], out_sem.at[i]))
    copy_all(steps)


def pick_kernel(ks, where, table, points, *refs):
    n = len(ks)
    outs, (asked, held, in_sem, out_sem) = refs[:n], refs[n:]
    pairs = table.shape[1] // 2
    me = where[0]
    for j, k in enumerate(ks):
        g = jnp.bitwise_xor(me, k)
        for c in range(CAP + 1):
            asked[c] = 0

        def look(p, found):
            asked[found] = table[g, pairs + p]
            return found + jnp.where(table[g, p] == me, 1, 0)

        lax.fori_loop(0, pairs, look, 0)
        for c in range(CAP):
            pltpu.make_async_copy(points.at[asked[c]], held.at[j, c], in_sem.at[j, c]).start()
    for j in range(n):
        for c in range(CAP):
            pltpu.make_async_copy(points.at[0], held.at[j, c], in_sem.at[j, c]).wait()
        pltpu.make_async_copy(held.at[j], outs[j], out_sem.at[j]).start()
    for j in range(n):
        pltpu.make_async_copy(held.at[j], outs[j], out_sem.at[j]).wait()


def column_kernel(ks, subs, own, chained, where, pair_at, live, partner, points, *refs):
    refs = list(refs)
    take = lambda n: [refs.pop(0) for _ in range(n)]
    owner, cols = take(subs), take(subs)
    arrived = take(len([k for k in ks if k]))
    if chained:
        take(2)
    back = take(len(ks))
    keep, send = take(2)
    vbuf, ubuf, cbuf, bbuf, in_sem, out_sem, strip_sem = refs
    strip = vbuf.shape[1]
    width = bbuf.shape[2]
    n = len(ks) * CAP
    me, sub = where[0], where[1]

    def pair_of(i):
        return pair_at[jnp.bitwise_xor(me, ks[i // CAP]), i % CAP]

    def fetch(i, do):
        k, c = ks[i // CAP], i % CAP
        p = pair_of(i)

        @pl.when(p >= 0)
        def _():
            o = lax.div(p, own)
            rel = jnp.bitwise_xor(o, sub)
            if k == 0:
                do(points.at[partner[0, p]], vbuf.at[i], in_sem.at[i, 0])
            else:
                do(arrived[[m for m in ks if m].index(k)].at[c], vbuf.at[i], in_sem.at[i, 0])
            for r in range(subs):
                spot = jnp.bitwise_xor(sub, r)
                span = pl.ds(pl.multiple_of(spot * strip, strip), strip)
                do(owner[r].at[p], ubuf.at[i, span], in_sem.at[i, 2 + r])

                @pl.when(rel == r)
                def _():
                    do(cols[r].at[p - o * own], cbuf.at[i], in_sem.at[i, 1])

    def pass_on(i, do):
        p = pair_of(i)

        @pl.when(p >= 0)
        def _():
            o = lax.div(p, own)
            rel = jnp.bitwise_xor(o, sub)
            low = jnp.bitwise_and(rel, 1)

            @pl.when(rel < 2)
            def _():
                do(vbuf.at[i], keep.at[low, p - o * own], strip_sem.at[i])

            @pl.when(rel >= 2)
            def _():
                do(vbuf.at[i], send.at[low, p - o * own], strip_sem.at[i])

    def start(a, b, s):
        pltpu.make_async_copy(a, b, s).start()

    def wait(a, b, s):
        pltpu.make_async_copy(a, b, s).wait()

    for i in range(n):
        fetch(i, start)
    for i in range(n):
        fetch(i, wait)
        pass_on(i, start)
        p = pair_of(i)

        @pl.when(p >= 0)
        def _():
            mask = lax.broadcasted_iota(jnp.int32, (1, width), 1) < live[jnp.maximum(p, 0)]
            tile = tile_of(vbuf[i], ubuf[i])
            part = jnp.dot(tile, cbuf[i], preferred_element_type=jnp.float32)
            bbuf[i] = (part * mask.astype(jnp.float32)).astype(jnp.bfloat16)

        @pl.when(p < 0)
        def _():
            bbuf[i] = jnp.zeros((strip, width), jnp.bfloat16)

        start(bbuf.at[i], back[i // CAP].at[i % CAP], out_sem.at[i])
    for i in range(n):
        wait(bbuf.at[i], back[i // CAP].at[i % CAP], out_sem.at[i])
        pass_on(i, wait)


def row_kernel(subs, own, where, live, keep, crossed, row_sketch, parts, *refs):
    owner = refs[:subs]
    mine, other, vbuf, ubuf, wbuf, rkeep, rsend, in_sem, out_sem = refs[subs:]
    strip, width = wbuf.shape[2], wbuf.shape[3]
    sub = where[1]
    n = 2 * own
    fetches = []
    for i in range(n):
        low, q = i // own, i % own
        p = jnp.bitwise_xor(sub, low) * own + q
        moves = [
            (keep.at[low, q], vbuf.at[i, pl.ds(0, strip)]),
            (crossed.at[low, q], vbuf.at[i, pl.ds(strip, strip)]),
        ]
        for half in range(2):
            if low == 0:
                spot = jnp.bitwise_xor(sub, 2 * half)
                span = pl.ds(pl.multiple_of(spot * strip, strip), strip)
                moves.append((row_sketch.at[0, q, span], wbuf.at[i, half]))
            else:
                moves.append((parts.at[half, q], wbuf.at[i, half]))
        for r in range(subs):
            spot = jnp.bitwise_xor(sub, r)
            span = pl.ds(pl.multiple_of(spot * strip, strip), strip)
            moves.append((owner[r].at[p], ubuf.at[i, span]))
        fetches.append([pltpu.make_async_copy(a, b, in_sem.at[i, j]) for j, (a, b) in enumerate(moves)])
    for f in fetches:
        for c in f:
            c.start()
    outs = []
    for i in reversed(range(n)):
        low, q = i // own, i % own
        p = jnp.bitwise_xor(sub, low) * own + q
        for c in fetches[i]:
            c.wait()
        mask = lax.broadcasted_iota(jnp.int32, (1, width), 1) < live[p]
        tile = tile_of(ubuf[i], vbuf[i])
        w = wbuf[i].reshape(2 * strip, width)
        part = jnp.dot(tile, w, preferred_element_type=jnp.float32) * mask.astype(jnp.float32)
        if low == 0:
            rkeep[q] = part
            outs.append(pltpu.make_async_copy(rkeep.at[q], mine.at[q], out_sem.at[i]))
        else:
            rsend[q] = part.astype(jnp.bfloat16)
            outs.append(pltpu.make_async_copy(rsend.at[q], other.at[q], out_sem.at[i]))
        outs[-1].start()
    for o in outs:
        o.wait()


def place_kernel(where, *refs):
    n = len(refs) - 4
    pieces, out, (held, in_sem, out_sem) = refs[:n], refs[n], refs[n + 1 :]
    me = where[0]
    copy_all(
        [
            (pieces[k], held.at[k], out.at[0, jnp.bitwise_xor(me, k)], in_sem.at[k], out_sem.at[k])
            for k in range(n)
        ]
    )


def shards(
    points, row_sketch, col_sketch, pair_count, pair_local, pair_src, pair_partner, pair_rank
):
    groups = lax.axis_size("clu")
    subs = lax.axis_size("sub")
    _, strip, dim = points.shape
    pairs = pair_src.shape[1]
    own = pairs // subs
    length, width = row_sketch.shape[2:]
    bf16, f32, i32 = jnp.bfloat16, jnp.float32, jnp.int32
    shape = jax.ShapeDtypeStruct
    dma = pltpu.SemaphoreType.DMA
    vmem = pltpu.VMEM
    where = jnp.stack([lax.axis_index("clu"), lax.axis_index("sub")]).astype(i32)

    def hop_clu(x, k):
        return lax.ppermute(x, "clu", [(g, g ^ k) for g in range(groups)])

    def hop_sub(x, r):
        return lax.ppermute(x, "sub", [(s, s ^ r) for s in range(subs)])

    row = jnp.concatenate([pair_src, pair_partner], axis=1)
    row = jnp.broadcast_to(row, (groups, 2 * pairs))
    table = lax.all_to_all(row, "clu", split_axis=0, concat_axis=0, tiled=True)
    pair_at, live = pl.pallas_call(
        functools.partial(table_kernel, groups),
        out_shape=(shape((groups, CAP), i32), shape((pairs,), i32)),
        in_specs=[SMEM] * 3,
        out_specs=(SMEM,) * 2,
        scratch_shapes=[pltpu.SMEM((groups,), i32)],
        name="tables",
    )(pair_src, pair_count, pair_rank)
    strips, parts = pl.pallas_call(
        prep_kernel,
        out_shape=(shape((pairs, strip, dim), bf16), shape((2, own, strip, width), bf16)),
        in_specs=[SMEM, SMEM, ANY, ANY],
        out_specs=(ANY, ANY),
        scratch_shapes=[
            vmem((pairs, strip, dim), bf16),
            vmem((2, own, strip, width), bf16),
            dma((pairs + 2,)),
            dma((pairs + 2,)),
        ],
        name="prep",
    )(where, pair_local, points, row_sketch)
    bits = [1 << b for b in reversed(range((subs - 1).bit_length()))]

    def spread(block):
        have = {0: block}
        for bit in bits:
            for r in list(have):
                have[r | bit] = hop_sub(have[r], bit)
        return [have[r] for r in range(subs)]

    cols = spread(col_sketch[0])
    owner = spread(strips)
    parts = hop_sub(parts, 1)

    far = groups // 2
    ks = [far, far + 1] + [k for k in range(1, groups) if k not in (far, far + 1)]
    chosen = pl.pallas_call(
        functools.partial(pick_kernel, ks),
        out_shape=[shape((CAP, strip, dim), bf16)] * len(ks),
        in_specs=[SMEM, SMEM, ANY],
        out_specs=[ANY] * len(ks),
        scratch_shapes=[
            pltpu.SMEM((CAP + 1,), i32),
            vmem((len(ks), CAP, strip, dim), bf16),
            dma((len(ks), CAP)),
            dma((len(ks),)),
        ],
        name="pick",
    )(where, table, points)
    arrived = {k: hop_clu(x, k) for k, x in zip(ks, chosen)}

    state = []
    back = {}
    sets = [[0] + ks[:2], ks[2:]] if groups <= 8 else [[0] + ks[:2]] + [ks[i : i + 5] for i in range(2, len(ks), 5)]
    for some in sets:
        n = len(some) * CAP
        operands = [where, pair_at, live, pair_partner, points, *owner, *cols]
        operands += [arrived[k] for k in some if k]
        specs = [SMEM] * 4 + [ANY] * (len(operands) - 4)
        alias = {len(operands) + j: len(some) + j for j in range(len(state))}
        held = shape((2, own, strip, dim), bf16)
        out = pl.pallas_call(
            functools.partial(column_kernel, some, subs, own, bool(state)),
            out_shape=[shape((CAP, strip, width), bf16)] * len(some) + [held, held],
            in_specs=specs + [ANY] * len(state),
            out_specs=[ANY] * (len(some) + 2),
            scratch_shapes=[
                vmem((n, strip, dim), bf16),
                vmem((n, length, dim), bf16),
                vmem((n, length, width), bf16),
                vmem((n, strip, width), bf16),
                dma((n, 2 + subs)),
                dma((n,)),
                dma((n,)),
            ],
            input_output_aliases=alias,
            name="columns_a" if not state else "columns_b",
        )(*operands, *state)
        back.update(zip(some, out))
        state = out[len(some) :]

    keep, send = state
    crossed = hop_sub(send, 2)
    mine, other = pl.pallas_call(
        functools.partial(row_kernel, subs, own),
        out_shape=(shape((own, length, width), f32), shape((own, length, width), bf16)),
        in_specs=[SMEM] * 2 + [ANY] * (4 + subs),
        out_specs=(ANY, ANY),
        scratch_shapes=[
            vmem((2 * own, 2 * strip, dim), bf16),
            vmem((2 * own, length, dim), bf16),
            vmem((2 * own, 2, strip, width), bf16),
            vmem((own, length, width), f32),
            vmem((own, length, width), bf16),
            dma((2 * own, 4 + subs)),
            dma((2 * own,)),
        ],
        name="rows",
    )(where, live, keep, crossed, row_sketch, parts, *owner)
    row_factor = (mine + hop_sub(other, 1).astype(f32)).astype(bf16)[None]

    pieces = [back[0]] + [hop_clu(back[k], k) for k in range(1, groups)]
    col_factor = pl.pallas_call(
        place_kernel,
        out_shape=shape((1, groups, CAP, strip, width), bf16),
        in_specs=[SMEM] + [ANY] * groups,
        out_specs=ANY,
        scratch_shapes=[vmem((groups, CAP, strip, width), bf16), dma((groups,)), dma((groups,))],
        name="place",
    )(where, *pieces)
    return (row_factor, col_factor)


def solution(mesh):
    placed = (
        P("clu", "sub", None),
        P("clu", "sub", None, None),
        P("clu", "sub", None, None),
        P("clu"),
        P("clu", None),
        P("clu", None),
        P("clu", None),
        P("clu", None),
    )
    return jax.shard_map(
        shards,
        mesh=mesh,
        in_specs=placed,
        out_specs=(P("clu", "sub", None, None), P("clu", None, None, "sub", None)),
        check_vma=False,
    )
```
